32 devices in a mesh: dp: 4 (over y, x), fsdp: 8 (over z, core).
Axes of the slice: x: 2, y: 2, z: 4, core: 2. Of those that a mesh axis runs over, the one named last changes fastest.
Arguments:
- tokens: bfloat16 [4096, 1536], P(('dp', 'fsdp')), may hold values from -6 to 6
- lengths: int32 [32], P(('dp', 'fsdp')), may hold values from 64 to 128, as said below
- positions: int32 [4096], P(('dp', 'fsdp')), may hold values from 0 to 4476, as said below
- conditioning: bfloat16 [4096, 768], P(('dp', 'fsdp')), may hold values from -6 to 6
- gain_one: bfloat16 [1536], P(('dp', 'fsdp')), may hold values from 0.5 to 1.5
- self_proj: bfloat16 [1536, 4608], P(('dp', 'fsdp')), may hold values from -0.15625 to 0.15625
- self_out: bfloat16 [1536, 1536], P(('dp', 'fsdp')), may hold values from -1.25 to 1.25
- gain_two: bfloat16 [1536], P(('dp', 'fsdp')), may hold values from 0.5 to 1.5
- cross_query: bfloat16 [1536, 1536], P(('dp', 'fsdp')), may hold values from -0.15625 to 0.15625
- cross_keyval: bfloat16 [768, 3072], P(('dp', 'fsdp')), may hold values from -0.21875 to 0.21875
- cross_out: bfloat16 [1536, 1536], P(('dp', 'fsdp')), may hold values from -0.875 to 0.875
- gain_three: bfloat16 [1536], P(('dp', 'fsdp')), may hold values from 0.5 to 1.5
- feed_in: bfloat16 [1536, 12288], P(('dp', 'fsdp')), may hold values from -0.15625 to 0.15625
- feed_bias: bfloat16 [12288], P(('dp', 'fsdp')), may hold values from -3 to 3
- feed_down: bfloat16 [6144, 1536], P(('dp', 'fsdp')), may hold values from -0.078125 to 0.078125
- down_bias: bfloat16 [1536], P(('dp', 'fsdp')), may hold values from -3 to 3
- cotangent: bfloat16 [4096, 1536], P(('dp', 'fsdp')), may hold values from -6 to 6
Outputs:
- output: bfloat16 [4096, 1536], P(('dp', 'fsdp'))
- tokens_grad: float32 [4096, 1536], P(('dp', 'fsdp'))
- gain_one_grad: float32 [1536], P(('dp', 'fsdp'))
- self_proj_grad: float32 [1536, 4608], P(('dp', 'fsdp'))
- self_out_grad: float32 [1536, 1536], P(('dp', 'fsdp'))
- gain_two_grad: float32 [1536], P(('dp', 'fsdp'))
- cross_query_grad: float32 [1536, 1536], P(('dp', 'fsdp'))
- cross_keyval_grad: float32 [768, 3072], P(('dp', 'fsdp'))
- cross_out_grad: float32 [1536, 1536], P(('dp', 'fsdp'))
- gain_three_grad: float32 [1536], P(('dp', 'fsdp'))
- feed_in_grad: float32 [1536, 12288], P(('dp', 'fsdp'))
- feed_bias_grad: float32 [12288], P(('dp', 'fsdp'))
- feed_down_grad: float32 [6144, 1536], P(('dp', 'fsdp'))
- down_bias_grad: float32 [1536], P(('dp', 'fsdp'))
The draws below stay inside these ranges and needn't reach their ends.
Inputs may be any that keep to these rules, and one draw needn't show every extreme that they name: `lengths`: each item's length is 64 or 128, and both occur. Within an item the positions rise from its first slot by a fixed stride of 1, 2 or 3.
All inputs are finite; a program needn't handle non-finite values.
Results may differ from the reference program's by a relative error of at most 0.022.
Values may be sent and summed in bfloat16 or wider, within the bound.
No kernel may reach another device: no remote copies, remote signals or barrier semaphores. Data moves between devices by JAX's collectives and lax.ppermute only.
A program may use at most 704 MiB of HBM per device.

```python
import jax
import jax.numpy as jnp
from jax import lax

D = 1536
HEADS = 24
HD = 64
FF = 6144
CD = 768
CTOK = 128
TOK_DEV = 128
ITEMS = 32
TOKENS = 4096


def draw_lengths(key, part):
    picks = jax.random.randint(key, (ITEMS,), 0, 2)
    picks = picks.at[0].set(1).at[1].set(0)
    return jnp.where(picks == 1, TOK_DEV, TOK_DEV // 2).astype(jnp.int32)


def draw_positions(key, part):
    key_start = jax.random.fold_in(key, 11)
    key_stride = jax.random.fold_in(key, 23)
    starts = jax.random.randint(key_start, (ITEMS,), 0, 4096)
    strides = jax.random.randint(key_stride, (ITEMS,), 1, 4)
    starts = starts.at[0].set(0).at[ITEMS - 1].set(4095)
    strides = strides.at[0].set(1).at[ITEMS - 1].set(3)
    slots = jnp.arange(TOK_DEV, dtype=jnp.int32)
    return (starts[:, None] + strides[:, None] * slots[None, :]).reshape(ITEMS * TOK_DEV).astype(jnp.int32)


def levels(key, extent, pieces, smallest, high):
    loudness = 1.0
    for axis_at, parts in pieces:
        steps = jax.random.uniform(jax.random.fold_in(jax.random.fold_in(key, 6), axis_at), (parts,), jnp.float32, smallest / len(pieces), high / len(pieces))
        loudness = loudness * jnp.repeat(jnp.exp(steps), extent[axis_at] // parts).reshape((-1,) + (1,) * (len(extent) - 1 - axis_at))
    return loudness


def noise(rng, extent, deviation, limit, cuts=(), held_as=jnp.bfloat16):
    values = deviation * jax.random.normal(rng, extent, jnp.float32)
    if cuts:
        values = values * levels(rng, extent, cuts, -0.22, 0.18)
    return jnp.clip(values, -limit, limit).astype(held_as)


def setup_inputs(seed: int = 0) -> dict:
    arg_keys = jax.random.split(jax.random.key(seed), 18)
    tokens = noise(arg_keys[0], (TOKENS, D), 1.0, 6.0, ((0, 32),))
    lengths = draw_lengths(jax.random.fold_in(arg_keys[17], 71), 0)
    positions = draw_positions(jax.random.fold_in(arg_keys[17], 71), 0)
    conditioning = noise(arg_keys[3], (ITEMS * CTOK, CD), 1.0, 6.0, ((0, 32),))
    gain_one = jnp.clip(1.0 + 0.1 * jax.random.normal(arg_keys[4], (D,), jnp.float32), 0.5, 1.5).astype(jnp.bfloat16)
    self_proj = noise(arg_keys[5], (D, 3 * D), D ** -0.5, 0.15625, ((0, 32),))
    self_out = noise(arg_keys[6], (D, D), (D // 64) ** -0.5, 1.25, ((0, 32),))
    gain_two = jnp.clip(1.0 + 0.1 * jax.random.normal(arg_keys[7], (D,), jnp.float32), 0.5, 1.5).astype(jnp.bfloat16)
    cross_query = noise(arg_keys[8], (D, D), D ** -0.5, 0.15625, ((0, 32),))
    cross_keyval = noise(arg_keys[9], (CD, 2 * D), CD ** -0.5, 0.21875, ((0, 32),))
    cross_out = noise(arg_keys[10], (D, D), (D // 32) ** -0.5, 0.875, ((0, 32),))
    gain_three = jnp.clip(1.0 + 0.1 * jax.random.normal(arg_keys[11], (D,), jnp.float32), 0.5, 1.5).astype(jnp.bfloat16)
    feed_in = noise(arg_keys[12], (D, 2 * FF), D ** -0.5, 0.15625, ((0, 32),))
    feed_bias = noise(arg_keys[13], (2 * FF,), 0.5, 3.0, ((0, 32),))
    feed_down = noise(arg_keys[14], (FF, D), FF ** -0.5, 0.078125, ((0, 32),))
    down_bias = noise(arg_keys[15], (D,), 0.5, 3.0, ((0, 32),))
    cotangent = noise(arg_keys[16], (TOKENS, D), 1.0, 6.0, ((0, 32),))
    return {"tokens": tokens, "lengths": lengths, "positions": positions, "conditioning": conditioning, "gain_one": gain_one, "self_proj": self_proj, "self_out": self_out, "gain_two": gain_two, "cross_query": cross_query, "cross_keyval": cross_keyval, "cross_out": cross_out, "gain_three": gain_three, "feed_in": feed_in, "feed_bias": feed_bias, "feed_down": feed_down, "down_bias": down_bias, "cotangent": cotangent}


@jax.custom_vjp
def low(v):
    return lax.optimization_barrier(v.astype(jnp.bfloat16)).astype(jnp.float32)

@jax.custom_vjp
def low_back(v):
    return v

def low_keep(v):
    return (low(v), None)

def low_pass(kept, grad):
    return (grad,)

def back_keep(v):
    return (v, None)

def back_low(kept, grad):
    return (low(grad),)
low.defvjp(low_keep, low_pass)
low_back.defvjp(back_keep, back_low)

def norm_rows(v, gain):
    centre = v - lax.optimization_barrier(jnp.mean(v, axis=-1, keepdims=True))
    spread = lax.optimization_barrier(jnp.mean(centre * centre, axis=-1, keepdims=True))
    return centre * lax.rsqrt(spread + 1e-05) * gain

def project(a, b):
    return jnp.einsum('gsd,de->gse', a, b, precision=lax.Precision.HIGHEST)

def rotate(t, places):
    quarter = t.shape[-1] // 4
    freq = 10000.0 ** (-jnp.arange(quarter, dtype=jnp.float32) / quarter)
    angle = places[..., None] * freq
    cosine = jnp.cos(angle)[:, :, None, :]
    sine = jnp.sin(angle)[:, :, None, :]
    first = t[..., :quarter]
    second = t[..., quarter:2 * quarter]
    return jnp.concatenate([first * cosine - second * sine, second * cosine + first * sine, t[..., 2 * quarter:]], axis=-1)

def attend(query, keys, values, mask):
    scores = low_back(jnp.einsum('gqhd,gkhd->ghqk', query, keys, precision=lax.Precision.HIGHEST) * 0.125)
    if mask is not None:
        scores = jnp.where(mask, scores, -1e+30)
    probs = low(jax.nn.softmax(scores, axis=-1))
    return low(low_back(jnp.einsum('ghqk,gkhd->gqhd', probs, values, precision=lax.Precision.HIGHEST)))

def group_layer(inputs, weights):
    block, lens, places, conds = inputs
    gain_one, self_proj, self_out, gain_two, cross_query, cross_keyval, cross_out, gain_three, feed_in, feed_bias, feed_down, down_bias = weights
    count, rows, width = block.shape
    h1 = low(norm_rows(block, gain_one))
    mixed = low_back(project(h1, self_proj))
    query = low(rotate(mixed[..., :width].reshape(count, rows, HEADS, HD), places))
    keys = low(rotate(mixed[..., width:2 * width].reshape(count, rows, HEADS, HD), places))
    values = low(mixed[..., 2 * width:].reshape(count, rows, HEADS, HD))
    live = jnp.arange(rows, dtype=jnp.int32)[None, :] < lens[:, None]
    attended = attend(query, keys, values, live[:, None, None, :]).reshape(count, rows, width)
    x1 = block + low_back(project(attended, self_out))
    h2 = low(norm_rows(x1, gain_two))
    query2 = low(low_back(project(h2, cross_query))).reshape(count, rows, HEADS, HD)
    keyval = low(low_back(project(conds, cross_keyval)))
    keys2 = keyval[..., :width].reshape(count, CTOK, HEADS, HD)
    values2 = keyval[..., width:].reshape(count, CTOK, HEADS, HD)
    attended2 = attend(query2, keys2, values2, None).reshape(count, rows, width)
    x2 = x1 + low_back(project(attended2, cross_out))
    h3 = low(norm_rows(x2, gain_three))
    z_pre = low_back(project(h3, feed_in) + feed_bias)
    value = z_pre[..., :FF]
    gate = z_pre[..., FF:]
    middle = low(value * jax.nn.silu(gate))
    return x2 + low_back(project(middle, feed_down) + down_bias)

def reference(tokens, lengths, positions, conditioning, gain_one, self_proj, self_out, gain_two, cross_query, cross_keyval, cross_out, gain_three, feed_in, feed_bias, feed_down, down_bias, cotangent):
    weights = tuple((w.astype(jnp.float32) for w in (gain_one, self_proj, self_out, gain_two, cross_query, cross_keyval, cross_out, gain_three, feed_in, feed_bias, feed_down, down_bias)))
    group = 8
    count = ITEMS // group
    whole_in = tokens.astype(jnp.float32)
    lens = lengths.reshape(count, group)
    places = positions.astype(jnp.float32).reshape(count, group, TOK_DEV)
    conds = conditioning.astype(jnp.float32).reshape(count, group, CTOK, CD)

    def forward(whole, params):
        blocks = whole.reshape(count, group, TOK_DEV, D)

        def step(carry, inputs):
            return (carry, group_layer(inputs, params))
        unused, outs = lax.scan(jax.checkpoint(step), jnp.zeros((), jnp.float32), (blocks, lens, places, conds))
        return outs.reshape(TOKENS, D)
    result, pullback = jax.vjp(forward, whole_in, weights)
    live = (jnp.arange(TOK_DEV, dtype=jnp.int32)[None, :] < lengths[:, None]).reshape(TOKENS, 1)
    grad = jnp.where(live, cotangent.astype(jnp.float32), jnp.float32(0.0))
    token_grad, grads = pullback(grad)
    return (result.astype(jnp.bfloat16), token_grad, grads[0], grads[1], grads[2], grads[3], grads[4], grads[5], grads[6], grads[7], grads[8], grads[9], grads[10], grads[11])
```

```python
import jax
import jax.numpy as jnp
from jax import lax
from jax.sharding import PartitionSpec as P

HEADS = 24
HD = 64
BF = jnp.bfloat16
FL = jnp.float32


def xor_perm(k, size):
    return [(i, i ^ k) for i in range(size)]


def across(v, k):
    return lax.ppermute(v, "dp", xor_perm(k, lax.axis_size("dp")))


def swap_core(v):
    return lax.ppermute(v, "fsdp", xor_perm(1, lax.axis_size("fsdp")))


def ring_next(v):
    nf = lax.axis_size("fsdp")
    return lax.ppermute(v, "fsdp", [(i, (i + 2) % nf) for i in range(nf)])


def place(buf, piece, starts):
    return lax.dynamic_update_slice(buf, piece.reshape(piece.shape), starts)


def gather_line(chunk):
    nf = lax.axis_size("fsdp")
    nz = nf // 2
    f = lax.axis_index("fsdp")
    z, c = f // 2, f % 2
    buf = jnp.zeros((nz, 2) + chunk.shape, chunk.dtype)
    v = chunk
    zero = (0,) * chunk.ndim
    for s in range(nz):
        if s:
            v = ring_next(v)
        u = swap_core(v)
        at = (z - s) % nz
        buf = lax.dynamic_update_slice(buf, v[None, None], (at, c) + zero)
        buf = lax.dynamic_update_slice(buf, u[None, None], (at, 1 - c) + zero)
    return buf


def reduce_line(parts):
    nf = lax.axis_size("fsdp")
    nz = nf // 2
    f = lax.axis_index("fsdp")
    z, c = f // 2, f % 2
    give = lax.dynamic_index_in_dim(parts, 1 - c, 1, keepdims=False)
    keep = lax.dynamic_index_in_dim(parts, c, 1, keepdims=False)
    got = swap_core(give)
    summed = (keep.astype(FL) + got.astype(FL)).astype(BF)
    acc = None
    for s in range(1, nz + 1):
        own = lax.dynamic_index_in_dim(summed, (z - s) % nz, 0, keepdims=False)
        acc = own.astype(FL) if acc is None else own.astype(FL) + acc.astype(FL)
        if s < nz:
            acc = ring_next(acc.astype(BF))
    return acc


def gather_dp(v):
    n = lax.axis_size("dp")
    t = lax.axis_index("dp")
    buf = jnp.zeros((n,) + v.shape, v.dtype)
    zero = (0,) * v.ndim
    for k in range(n):
        got = across(v, k) if k else v
        buf = lax.dynamic_update_slice(buf, got[None], (t ^ k,) + zero)
    return buf


def reduce_dp(parts):
    n = lax.axis_size("dp")
    t = lax.axis_index("dp")
    low = parts.astype(BF)
    acc = lax.dynamic_index_in_dim(parts, t, 0, keepdims=False)
    for k in range(1, n):
        got = across(lax.dynamic_index_in_dim(low, t ^ k, 0, keepdims=False), k)
        acc = acc + got.astype(FL)
    return acc


def swap_dp(v):
    n = lax.axis_size("dp")
    t = lax.axis_index("dp")
    buf = jnp.zeros(v.shape, v.dtype)
    zero = (0,) * (v.ndim - 1)
    for k in range(n):
        got = lax.dynamic_slice_in_dim(v, t ^ k, 1, 0)
        if k:
            got = across(got, k)
        buf = lax.dynamic_update_slice(buf, got, (t ^ k,) + zero)
    return buf


def columns_of(weight, sections):
    n = lax.axis_size("dp")
    rows, width = weight.shape
    share = width // sections // n
    cut = lambda s, j: weight[:, s * n * share + j * share : s * n * share + (j + 1) * share]
    return jnp.stack([jnp.concatenate([cut(s, j) for s in range(sections)], axis=1) for j in range(n)])


def columns_back(parts, sections):
    n, rows, width = parts.shape
    share = width // sections
    return jnp.concatenate(
        [parts[j, :, s * share : (s + 1) * share] for s in range(sections) for j in range(n)], axis=1
    )


def gather_columns(weight, sections):
    chunk = swap_dp(columns_of(weight, sections))
    full = gather_line(chunk)
    n, rows, width = chunk.shape
    return full.transpose(2, 0, 1, 3, 4).reshape(-1, width)


def gather_rows(weight):
    return gather_line(weight).reshape(-1, weight.shape[1])


def reduce_columns(grad, sections):
    n = lax.axis_size("dp")
    nf = lax.axis_size("fsdp")
    width = grad.shape[1]
    parts = grad.astype(BF).reshape(n, nf // 2, 2, -1, width).transpose(1, 2, 0, 3, 4)
    mine = reduce_line(parts).astype(BF)
    return columns_back(swap_dp(mine).astype(FL), sections)


def reduce_rows(grad):
    nf = lax.axis_size("fsdp")
    return reduce_line(grad.astype(BF).reshape(nf // 2, 2, -1, grad.shape[1]))


def norm_rows(v, gain):
    centre = v - jnp.mean(v, axis=-1, keepdims=True)
    rstd = lax.rsqrt(jnp.mean(centre * centre, axis=-1, keepdims=True) + 1e-05)
    unit = centre * rstd
    return unit * gain, unit, rstd


def norm_back(grad, gain, unit, rstd):
    scaled = grad * gain
    return rstd * (
        scaled
        - jnp.mean(scaled, axis=-1, keepdims=True)
        - unit * jnp.mean(scaled * unit, axis=-1, keepdims=True)
    )


def outer_sum(left, right):
    return lax.dot_general(left, right, (((0,), (0,)), ((), ())), preferred_element_type=FL)


def back_mul(grad, weight):
    return lax.dot_general(grad, weight, (((1,), (1,)), ((), ())), preferred_element_type=FL)


def mul(a, b):
    return jnp.dot(a, b, preferred_element_type=FL)


def rotate(t, cosine, sine):
    quarter = cosine.shape[-1]
    first = t[..., :quarter]
    second = t[..., quarter : 2 * quarter]
    return jnp.concatenate(
        [first * cosine - second * sine, second * cosine + first * sine, t[..., 2 * quarter :]], axis=-1
    )


def raw_scores(query, keys, mask):
    scores = jnp.einsum("gqhd,gkhd->ghqk", query, keys, preferred_element_type=FL) * 0.125
    if mask is not None:
        scores = jnp.where(mask, scores, -1e30)
    return scores


def attend(query, keys, values, mask):
    scores = raw_scores(query, keys, mask)
    top = jnp.max(scores, axis=-1, keepdims=True)
    weight = jnp.exp(scores - top)
    total = jnp.sum(weight, axis=-1, keepdims=True)
    probs = (weight / total).astype(BF)
    result = jnp.einsum("ghqk,gkhd->gqhd", probs, values, preferred_element_type=FL)
    return result, top + jnp.log(total)


def attend_back(query, keys, values, mask, lse, grad_out):
    probs = jnp.exp(raw_scores(query, keys, mask) - lse)
    dprob = jnp.einsum("gqhd,gkhd->ghqk", grad_out, values, preferred_element_type=FL)
    dvalues = jnp.einsum("ghqk,gqhd->gkhd", probs.astype(BF), grad_out, preferred_element_type=FL)
    delta = jnp.sum(dprob * probs, axis=-1, keepdims=True)
    dscore = (probs * (dprob - delta)).astype(BF)
    dquery = jnp.einsum("ghqk,gkhd->gqhd", dscore, keys, preferred_element_type=FL) * 0.125
    dkeys = jnp.einsum("ghqk,gqhd->gkhd", dscore, query, preferred_element_type=FL) * 0.125
    return dquery, dkeys, dvalues


def per_device(
    tokens,
    lengths,
    positions,
    conditioning,
    gain_one,
    self_proj,
    self_out,
    gain_two,
    cross_query,
    cross_keyval,
    cross_out,
    gain_three,
    feed_in,
    feed_bias,
    feed_down,
    down_bias,
    cotangent,
):
    rows, width = tokens.shape
    n, nf = lax.axis_size("dp"), lax.axis_size("fsdp")
    t, f = lax.axis_index("dp"), lax.axis_index("fsdp")
    crows, cwidth = conditioning.shape
    heads = HEADS // n
    hw = heads * HD
    owner = lambda a, b: (b // (nf // 2)) * (n * nf // 2) + a * (nf // 2) + b % (nf // 2)
    to_rank = [(owner(a, b), a * nf + b) for a in range(n) for b in range(nf)]
    to_owner = [(b, a) for a, b in to_rank]

    small = gather_dp(jnp.concatenate([gain_one, gain_two, gain_three, down_bias]))
    bias_piece = lax.ppermute(feed_bias, ("dp", "fsdp"), to_rank)
    every = gather_line(jnp.concatenate([small.reshape(-1), bias_piece]))
    share = gain_one.shape[0]
    vectors = every[:, :, : n * 4 * share].reshape(nf, n, 4, share).transpose(2, 1, 0, 3).reshape(4, width)
    g_one, g_two, g_three, b_down = vectors.astype(FL)
    b_in = every[:, :, n * 4 * share :].reshape(-1).astype(FL)

    info = gather_dp(jnp.concatenate([positions, jnp.broadcast_to(lengths, (rows,))]).reshape(2, rows))
    places = info[:, 0]
    live_all = jnp.arange(rows, dtype=jnp.int32)[None, :] < info[:, 1]
    key_mask = live_all[:, None, None, :]
    quarter = HD // 4
    freq = 10000.0 ** (-jnp.arange(quarter, dtype=FL) / quarter)
    angle = places.astype(FL)[:, :, None] * freq
    cosine = jnp.cos(angle)[:, :, None, :]
    sine = jnp.sin(angle)[:, :, None, :]

    w_proj = gather_columns(self_proj, 3)
    w_out = gather_rows(self_out)
    w_query = gather_columns(cross_query, 1)
    w_keyval = gather_columns(cross_keyval, 2)
    w_cross = gather_rows(cross_out)
    w_in = gather_columns(feed_in, 2)
    w_down = gather_rows(feed_down)

    live = jnp.arange(rows, dtype=jnp.int32) < lengths[0]
    grad = jnp.where(live[:, None], cotangent.astype(FL), 0.0)
    grad_all = gather_dp(grad.astype(BF)).reshape(n * rows, width)
    cond_all = gather_dp(conditioning).reshape(n * crows, cwidth)

    x_start = tokens.astype(FL)
    h_one, unit_one, rstd_one = norm_rows(x_start, g_one)
    h_one = gather_dp(h_one.astype(BF)).reshape(n * rows, width)
    mixed = mul(h_one, w_proj).reshape(n, rows, 3, heads, HD)
    query = rotate(mixed[:, :, 0], cosine, sine).astype(BF)
    keys = rotate(mixed[:, :, 1], cosine, sine).astype(BF)
    values = mixed[:, :, 2].astype(BF)
    attended, lse_one = attend(query, keys, values, key_mask)
    attended = attended.reshape(n * rows, hw).astype(BF)
    x_one = x_start + reduce_dp(mul(attended, w_out).reshape(n, rows, width))

    h_two, unit_two, rstd_two = norm_rows(x_one, g_two)
    h_two = gather_dp(h_two.astype(BF)).reshape(n * rows, width)
    query_two = mul(h_two, w_query).astype(BF).reshape(n, rows, heads, HD)
    keyval = mul(cond_all, w_keyval).astype(BF).reshape(n, crows, 2, heads, HD)
    keys_two, values_two = keyval[:, :, 0], keyval[:, :, 1]
    attended_two, lse_two = attend(query_two, keys_two, values_two, None)
    attended_two = attended_two.reshape(n * rows, hw).astype(BF)
    x_two = x_one + reduce_dp(mul(attended_two, w_cross).reshape(n, rows, width))

    h_three, unit_three, rstd_three = norm_rows(x_two, g_three)
    h_three = gather_dp(h_three.astype(BF)).reshape(n * rows, width)
    hidden = w_in.shape[1] // 2
    z_pre = mul(h_three, w_in) + b_in
    value, gate = z_pre[:, :hidden], z_pre[:, hidden:]
    sig = jax.nn.sigmoid(gate)
    middle = (value * gate * sig).astype(BF)
    result = x_two + reduce_dp(mul(middle, w_down).reshape(n, rows, width)) + b_down
    output = result.astype(BF)
    down_grad = reduce_rows(outer_sum(middle, grad_all))
    dmiddle = back_mul(grad_all, w_down)
    dvalue = dmiddle * gate * sig
    dgate = dmiddle * value * sig * (1.0 + gate * (1.0 - sig))
    dz = jnp.concatenate([dvalue, dgate], axis=1).astype(BF)
    in_grad = reduce_columns(outer_sum(h_three, dz), 2)
    dh_three = reduce_dp(back_mul(dz, w_in).reshape(n, rows, width))
    dx_two = grad + norm_back(dh_three, g_three, unit_three, rstd_three)

    down_cols = jnp.sum(grad_all.astype(FL), axis=0).reshape(n, nf, share)
    down_cols = lax.dynamic_index_in_dim(down_cols, t, 0, keepdims=False)
    in_cols = jnp.sum(dz.astype(FL), axis=0).reshape(nf, -1)
    cols = jnp.concatenate([in_cols, down_cols], axis=1).reshape(nf // 2, 2, -1)
    cols = reduce_line(cols.astype(BF))
    dbias_grad = cols[in_cols.shape[1] :]
    bias_grad = lax.ppermute(cols[: in_cols.shape[1]], ("dp", "fsdp"), to_owner)

    d_two = gather_dp(dx_two.astype(BF)).reshape(n * rows, width)
    cross_grad = reduce_rows(outer_sum(attended_two, d_two))
    da_two = back_mul(d_two, w_cross).astype(BF).reshape(n, rows, heads, HD)
    dq_two, dk_two, dv_two = attend_back(query_two, keys_two, values_two, None, lse_two, da_two)
    dq_low = dq_two.reshape(n * rows, hw).astype(BF)
    dkeyval = jnp.concatenate(
        [dk_two.reshape(n * crows, hw), dv_two.reshape(n * crows, hw)], axis=1
    ).astype(BF)
    query_grad = reduce_columns(outer_sum(h_two, dq_low), 1)
    keyval_grad = reduce_columns(outer_sum(cond_all, dkeyval), 2)
    dh_two = reduce_dp(back_mul(dq_low, w_query).reshape(n, rows, width))
    dx_one = dx_two + norm_back(dh_two, g_two, unit_two, rstd_two)

    d_one = gather_dp(dx_one.astype(BF)).reshape(n * rows, width)
    out_grad = reduce_rows(outer_sum(attended, d_one))
    da_one = back_mul(d_one, w_out).astype(BF).reshape(n, rows, heads, HD)
    dq_one, dk_one, dv_one = attend_back(query, keys, values, key_mask, lse_one, da_one)
    dq_one = rotate(dq_one, cosine, -sine)
    dk_one = rotate(dk_one, cosine, -sine)
    dmixed = jnp.concatenate(
        [v.reshape(n * rows, hw) for v in (dq_one, dk_one, dv_one)], axis=1
    ).astype(BF)
    proj_grad = reduce_columns(outer_sum(h_one, dmixed), 3)
    dh_one = reduce_dp(back_mul(dmixed, w_proj).reshape(n, rows, width))
    tokens_grad = dx_one + norm_back(dh_one, g_one, unit_one, rstd_one)

    def gain_grad(weight, weight_grad, gain):
        return jnp.sum(weight.astype(FL) * weight_grad, axis=1) / gain.astype(FL)

    return (
        output,
        tokens_grad,
        gain_grad(self_proj, proj_grad, gain_one),
        proj_grad,
        out_grad,
        gain_grad(cross_query, query_grad, gain_two),
        query_grad,
        keyval_grad,
        cross_grad,
        gain_grad(feed_in, in_grad, gain_three),
        in_grad,
        bias_grad,
        down_grad,
        dbias_grad,
    )


def solution(mesh):
    both = ("dp", "fsdp")
    row, flat = P(both, None), P(both)
    return jax.shard_map(
        per_device,
        mesh=mesh,
        in_specs=(row, flat, flat, row, flat, row, row, flat, row, row, row, flat, row, flat, row, flat, row),
        out_specs=(row, row, flat, row, row, flat, row, row, row, flat, row, flat, row, flat),
        check_vma=False,
    )
```
